32 devices in a mesh: section: 4 (over x, core), seq: 8 (over z, y).
Axes of the slice: x: 2, y: 2, z: 4, core: 2. Of those that a mesh axis runs over, the one named last changes fastest.
Arguments:
- queries: bfloat16 [4, 2048, 3072], P('section', 'seq'), may hold values from -0.75 to 0.75
- out_grads: bfloat16 [4, 2048, 3072], P('section', 'seq'), may hold values from -0.59765625 to 0.59765625
- logsumexp: float32 [4, 24, 2048], P('section', None, 'seq'), may hold values from 3.5 to 5.5
- shared_keys: bfloat16 [128, 1024], P('seq'), may hold values from -48 to 48
- shared_values: bfloat16 [128, 1024], P('seq'), may hold values from -6 to 6
- query_starts: int32 [8], P('seq'), may hold values from 0 to 2047, as said below
- slab_starts: int32 [8], P('seq'), may hold values from 0 to 2047, as said below
Outputs:
- query_grads: float32 [4, 2048, 3072], P('section', 'seq')
- key_grads: float32 [128, 1024], P('seq', 'section')
- value_grads: float32 [128, 1024], P('seq', 'section')
The draws below stay inside these ranges and needn't reach their ends.
Inputs may be any that keep to these rules, and one draw needn't show every extreme that they name: s * 256 <= query_starts[s] < (s + 1) * 256. j * 256 <= slab_starts[j] < (j + 1) * 256.
All inputs are finite; a program needn't handle non-finite values.
Results may differ from the reference program's by a relative error of at most 0.004.
Values may be sent and summed in bfloat16 or wider, within the bound.
A program may use at most 128 MiB of HBM per device.

```python
import jax
import jax.numpy as jnp
from jax import lax

Q_HEADS = 24
KV_HEADS = 8
HEAD_DIM = 128
QDEV = 256
SLAB = 16
LAYERS = 4
SLABS = 8
QTOT = 2048
KTOT = 128


def draw_query_starts(key, part):
    shard_base = jnp.arange(SLABS, dtype=jnp.int32) * QDEV
    jitter = jax.random.randint(jax.random.fold_in(key, 11), (SLABS,), 0, QDEV, dtype=jnp.int32)
    jitter = jitter.at[0].set(0).at[SLABS - 1].set(QDEV - 1)
    return shard_base + jitter


def draw_slab_starts(key, part):
    shard_base = jnp.arange(SLABS, dtype=jnp.int32) * QDEV
    jitter = jax.random.randint(jax.random.fold_in(key, 23), (SLABS,), 0, QDEV, dtype=jnp.int32)
    jitter = jitter.at[0].set(0).at[SLABS - 1].set(QDEV - 1)
    return shard_base + jitter


def levels(stream_key, extent, shards, smallest, top_value):
    def one(axis_at, parts):
        draws = jax.random.uniform(jax.random.fold_in(jax.random.fold_in(stream_key, 6), axis_at), (parts,), jnp.float32, smallest / len(shards), top_value / len(shards))
        return jnp.repeat(jnp.exp(draws), extent[axis_at] // parts).reshape((-1,) + (1,) * (len(extent) - axis_at - 1))

    level = one(*shards[0])
    for cut in shards[1:]:
        level = level * one(*cut)
    return level


def gaussian(stream_key, shape, width, reach, cuts=(), kind=jnp.bfloat16):
    level = levels(stream_key, shape, cuts, -0.22, 0.18) if cuts else 1.0
    drawn = jax.random.normal(stream_key, shape, jnp.float32) * width * level
    return jnp.minimum(jnp.maximum(drawn, -reach), reach).astype(kind)


def setup_inputs(seed: int = 0) -> dict:
    key_list = jax.random.split(jax.random.key(seed), 8)
    queries = gaussian(key_list[0], (LAYERS, QTOT, Q_HEADS * HEAD_DIM), 0.125, 0.75, ((0, 4), (1, 8)))
    out_grads = gaussian(key_list[1], (LAYERS, QTOT, Q_HEADS * HEAD_DIM), 0.1, 0.59765625, ((0, 4), (1, 8)))
    logsumexp = jnp.clip(3.5 + 2.0 * jax.random.uniform(key_list[2], (LAYERS, Q_HEADS, QTOT), jnp.float32) ** levels(key_list[2], (LAYERS, Q_HEADS, QTOT), ((0, 4), (2, 8)), -0.2, 0.2), 3.5, 5.5)
    shared_keys = gaussian(key_list[3], (KTOT, KV_HEADS * HEAD_DIM), 8.0, 48.0, ((0, 8),))
    shared_values = gaussian(key_list[4], (KTOT, KV_HEADS * HEAD_DIM), 1.0, 6.0, ((0, 8),))
    query_starts = draw_query_starts(jax.random.fold_in(key_list[7], 71), 0)
    slab_starts = draw_slab_starts(jax.random.fold_in(key_list[7], 71), 0)
    return dict(queries=queries, out_grads=out_grads, logsumexp=logsumexp, shared_keys=shared_keys, shared_values=shared_values, query_starts=query_starts, slab_starts=slab_starts)


def round_half(values_in):
    rounded = values_in.astype(jnp.bfloat16)
    rounded = lax.optimization_barrier(rounded)
    return rounded.astype(jnp.float32)


def reference(queries, out_grads, logsumexp, shared_keys, shared_values, query_starts, slab_starts):
    score_scale = HEAD_DIM ** -0.5
    group_size = Q_HEADS // KV_HEADS
    query_pos = (query_starts[:, None] + jnp.arange(QDEV, dtype=jnp.int32)[None, :]).astype(jnp.int32)
    key_pos = (slab_starts[:, None] + jnp.arange(SLAB, dtype=jnp.int32)[None, :]).reshape(-1).astype(jnp.int32)
    key_grads = jnp.zeros((KTOT, KV_HEADS * HEAD_DIM), jnp.float32)
    value_grads = jnp.zeros((KTOT, KV_HEADS * HEAD_DIM), jnp.float32)
    layer_grads = []
    for layer_index in range(LAYERS):
        query_all = queries[layer_index].astype(jnp.float32).reshape(SLABS, QDEV, Q_HEADS, HEAD_DIM)
        grad_all = out_grads[layer_index].astype(jnp.float32).reshape(SLABS, QDEV, Q_HEADS, HEAD_DIM)
        saved_all = jnp.transpose(logsumexp[layer_index].reshape(Q_HEADS, SLABS, QDEV), (1, 0, 2))
        query_cols = []
        key_cols = []
        value_cols = []
        for head_index in range(KV_HEADS):
            low = head_index * group_size
            key_head = shared_keys[:, head_index * HEAD_DIM:(head_index + 1) * HEAD_DIM].astype(jnp.float32)
            value_head = shared_values[:, head_index * HEAD_DIM:(head_index + 1) * HEAD_DIM].astype(jnp.float32)

            def block_step(packed):
                query_group, grad_group, saved, rows_pos = packed
                visible = key_pos[None, :] <= rows_pos[:, None]
                scores = jnp.einsum('rhd,kd->hrk', query_group, key_head) * score_scale
                probs = jnp.where(visible[None], jnp.exp(scores - saved[:, :, None]), 0.0)
                grad_probs = jnp.einsum('rhd,kd->hrk', grad_group, value_head)
                row_delta = jnp.sum(probs * grad_probs, axis=2, keepdims=True)
                grad_scores = probs * (grad_probs - row_delta)
                probs_half = round_half(probs)
                scores_half = round_half(grad_scores)
                value_piece = jnp.einsum('hrk,rhd->kd', probs_half, grad_group)
                key_piece = jnp.einsum('hrk,rhd->kd', scores_half, query_group) * score_scale
                query_piece = (jnp.einsum('hrk,kd->rhd', scores_half, key_head) * score_scale).reshape(QDEV, group_size * HEAD_DIM)
                return query_piece, key_piece, value_piece

            query_blocks, key_blocks, value_blocks = lax.map(block_step, (query_all[:, :, low:low + group_size], grad_all[:, :, low:low + group_size], saved_all[:, low:low + group_size], query_pos))
            query_cols.append(query_blocks.reshape(QTOT, group_size * HEAD_DIM))
            key_cols.append(jnp.sum(key_blocks, axis=0))
            value_cols.append(jnp.sum(value_blocks, axis=0))
        layer_grads.append(jnp.concatenate(query_cols, axis=1))
        key_grads = key_grads + jnp.concatenate(key_cols, axis=1)
        value_grads = value_grads + jnp.concatenate(value_cols, axis=1)
    return jnp.stack(layer_grads), key_grads, value_grads
```

```python
import functools

import jax
import jax.numpy as jnp
from jax import lax
from jax.experimental import pallas as pl
from jax.experimental.pallas import tpu as pltpu
from jax.sharding import PartitionSpec as P

Q_HEADS = 24
KV_HEADS = 8
HEAD_DIM = 128
GROUP = Q_HEADS // KV_HEADS
SCALE = HEAD_DIM ** (-0.5)
LOG2E = 1.4426950408889634
HIDDEN = -1e30
FAR = 2**30
WRITES = 4
MESH = pl.DeviceIdType.MESH


def inner_factor(size):
    factor = 1
    while size % (2 * factor) == 0 and (2 * factor) ** 2 <= size:
        factor *= 2
    return factor


def contract(left, right, left_dim, right_dim):
    return lax.dot_general(
        left, right, (((left_dim,), (right_dim,)), ((), ())), preferred_element_type=jnp.float32
    )


def arrived(ref, sem):
    pltpu.make_async_copy(ref, ref, sem).wait()


def all_arrived(ref, sem, count, counts):
    for size in counts:

        @pl.when(count == size)
        def _():
            arrived(ref.at[pl.ds(0, size)], sem)


def order_of(inner):
    turns = KV_HEADS // inner
    order = []
    for turn in range(turns + 1):
        if turn < turns:
            order += [(turn, away) for away in range(1, inner)]
        if turn > 0 or inner == 1:
            order.append((turn - (inner > 1), 0))
    return order[:KV_HEADS]


def kernel(
    sections, shards, q_hbm, g_hbm, lse_hbm, k_hbm, v_hbm, q_start_hbm, k_start_hbm,
    dq_all, dk_out, dv_out,
    q_all, g_all, lse_all, pairs, starts, bias, ds_all, part_out, part_in, sum_out, sum_in, q_start, k_start,
    load_sem, pair_sem, start_send, start_recv, pair_send, pair_recv,
    hop_send, hop_recv, part_send, part_recv, sum_send, sum_recv, side_ready,
):
    inner = inner_factor(sections)
    outer = sections // inner
    turns = KV_HEADS // inner
    per_section = KV_HEADS // sections
    rows = q_all.shape[0]
    slab = pairs.shape[3]
    total_keys = shards * slab
    section, me = lax.axis_index("section"), lax.axis_index("seq")
    side, core = section // inner, lax.rem(section, inner)
    seen = jnp.minimum(me + 2, shards)
    reader = jnp.maximum(me - 1, 0)

    def owner_side(turn):
        return turn // per_section

    def block_of(turn):
        return turn % per_section

    def head_of(turn, away):
        owner = owner_side(turn) * inner + lax.rem(core + away, inner)
        return owner * per_section + block_of(turn)

    def across(away):
        return (lax.rem(side + away, outer) * inner + core, me)

    def partner(away):
        return (side * inner + lax.rem(core + away, inner), me)

    first = 1 % inner
    barrier = pltpu.get_barrier_semaphore()

    @pl.loop(0, seen)
    def _(owner):
        @pl.when(owner != me)
        def _():
            pl.semaphore_signal(barrier, inc=1, device_id=(section, owner), device_id_type=MESH)

    for away in range(1, inner):
        pl.semaphore_signal(barrier, inc=1, device_id=partner(away), device_id_type=MESH)
    for away in range(1, outer):
        pl.semaphore_signal(barrier, inc=1, device_id=across(away), device_id_type=MESH)

    place_load = pltpu.make_async_copy(k_start_hbm, k_start, load_sem.at[4])
    place_load.start()
    for turn in range(turns):
        head = head_of(turn, first)
        columns = pl.ds(pl.multiple_of(head * HEAD_DIM, HEAD_DIM), HEAD_DIM)
        pltpu.make_async_copy(k_hbm.at[:, columns], pairs.at[head, me, 0], pair_sem).start()
        pltpu.make_async_copy(v_hbm.at[:, columns], pairs.at[head, me, 1], pair_sem).start()

    loads = [
        pltpu.make_async_copy(q_hbm.at[0], q_all, load_sem.at[0]),
        pltpu.make_async_copy(g_hbm.at[0], g_all, load_sem.at[1]),
        pltpu.make_async_copy(lse_hbm.at[0], lse_all, load_sem.at[2]),
        pltpu.make_async_copy(q_start_hbm, q_start, load_sem.at[3]),
    ]
    for load in loads:
        load.start()

    @pl.loop(seen, shards)
    def _(owner):
        starts[owner] = jnp.full((1, rows), FAR, jnp.int32)
        for turn in range(turns):
            pairs[head_of(turn, first), owner] = jnp.zeros(pairs.shape[2:], pairs.dtype)

    @pl.loop(0, reader)
    def _(source):
        for block in range(per_section):
            for place in range(outer):
                sum_in[block, place * shards + source] = jnp.zeros(sum_in.shape[2:], sum_in.dtype)

    place_load.wait()
    starts[me] = jnp.full((1, rows), k_start[0], jnp.int32)
    mine = pairs.at[pl.ds(0, turns), 0]
    pltpu.make_async_copy(mine, mine, pair_sem).wait()
    pl.semaphore_wait(barrier, shards - reader - 1 + inner - 1 + outer - 1)

    def to_readers(send):
        @pl.loop(0, shards - reader)
        def _(turned):
            reading = shards - 1 - turned

            @pl.when(reading != me)
            def _():
                send(reading)

    for turn in range(turns):
        head = head_of(turn, first)

        @to_readers
        def _(reading):
            pltpu.make_async_remote_copy(
                src_ref=pairs.at[head, me],
                dst_ref=pairs.at[head, me],
                send_sem=pair_send.at[turn],
                recv_sem=pair_recv.at[turn],
                device_id=(section, reading),
                device_id_type=MESH,
            ).start()

        if turn == 0:
            @to_readers
            def _(reading):
                pltpu.make_async_remote_copy(
                    src_ref=starts.at[me],
                    dst_ref=starts.at[me],
                    send_sem=start_send,
                    recv_sem=start_recv,
                    device_id=(section, reading),
                    device_id_type=MESH,
                ).start()

    def take(turn, away):
        head = head_of(turn, away)
        if away != first:
            arrived(pairs.at[head], hop_recv.at[turn, away])
            return

        all_arrived(pairs.at[head], pair_recv.at[turn], seen - 1, range(1, shards))

        for forward in range(1, inner):
            pltpu.make_async_remote_copy(
                src_ref=pairs.at[head],
                dst_ref=pairs.at[head],
                send_sem=hop_send.at[turn, forward],
                recv_sem=hop_recv.at[turn, (first - forward) % inner],
                device_id=partner(forward),
                device_id_type=MESH,
            ).start()

    def columns_of(query_head):
        return pl.ds(pl.multiple_of(query_head * HEAD_DIM, HEAD_DIM), HEAD_DIM)

    def front(turn, away):
        head = head_of(turn, away)
        keys = pairs[head, :, 0].reshape(total_keys, HEAD_DIM)
        values = pairs[head, :, 1].reshape(total_keys, HEAD_DIM)
        products = []
        for member in range(GROUP):
            columns = columns_of(head * GROUP + member)
            products.append((contract(keys, q_all[:, columns], 1, 1), contract(values, g_all[:, columns], 1, 1)))
        return products

    def back(turn, away, products):
        head = head_of(turn, away)
        hidden = bias[...].reshape(total_keys, rows)
        all_probs, all_scores, queries, grads = [], [], [], []
        for member in range(GROUP):
            query_head = head * GROUP + member
            scores, grad_probs = products[member]
            probs = jnp.exp2(scores * (SCALE * LOG2E) + (hidden - lse_all[pl.ds(query_head, 1), :] * LOG2E))
            delta = jnp.sum(probs * grad_probs, axis=0, keepdims=True)
            scores_half = (probs * (grad_probs - delta)).astype(jnp.bfloat16)
            ds_all[query_head] = scores_half
            all_probs.append(probs.astype(jnp.bfloat16))
            all_scores.append(scores_half)
            queries.append(q_all[:, columns_of(query_head)])
            grads.append(g_all[:, columns_of(query_head)])
        key_part = contract(jnp.concatenate(all_scores, 1), jnp.concatenate(queries, 0), 1, 0)
        value_part = contract(jnp.concatenate(all_probs, 1), jnp.concatenate(grads, 0), 1, 0)
        return key_part.reshape(shards, slab, HEAD_DIM), value_part.reshape(shards, slab, HEAD_DIM)

    def hand_in(turn, away, key_part, value_part):
        part_out[turn, away - 1, :, 0] = key_part.astype(jnp.bfloat16)
        part_out[turn, away - 1, :, 1] = value_part.astype(jnp.bfloat16)
        pltpu.make_async_remote_copy(
            src_ref=part_out.at[turn, away - 1],
            dst_ref=part_in.at[turn, away - 1],
            send_sem=part_send.at[turn, away - 1],
            recv_sem=part_recv.at[turn, away - 1],
            device_id=partner(away),
            device_id_type=MESH,
        ).start()

    def pass_on(turn, key_part, value_part):
        for away in range(1, inner):
            arrived(part_in.at[turn, away - 1], part_recv.at[turn, away - 1])
            key_part = key_part + part_in[turn, away - 1, :, 0].astype(jnp.float32)
            value_part = value_part + part_in[turn, away - 1, :, 1].astype(jnp.float32)
        sum_out[turn, :, 0] = key_part.astype(jnp.bfloat16)
        sum_out[turn, :, 1] = value_part.astype(jnp.bfloat16)
        target = owner_side(turn)
        block = block_of(turn)

        @pl.loop(0, seen)
        def _(owner):
            @pl.when((owner != me) | (target != side))
            def _():
                pltpu.make_async_remote_copy(
                    src_ref=sum_out.at[turn, owner],
                    dst_ref=sum_in.at[block, side * shards + me],
                    send_sem=sum_send.at[turn],
                    recv_sem=sum_recv.at[block],
                    device_id=(target * inner + core, owner),
                    device_id_type=MESH,
                ).start()

        @pl.when(target == side)
        def _():
            sum_in[block, side * shards + me] = sum_out[turn, me]

    order = order_of(inner)
    take(*order[0])

    all_arrived(starts, start_recv, seen - 1, range(1, shards))

    for away in range(1, outer):
        pl.semaphore_signal(side_ready, inc=1, device_id=across(away), device_id_type=MESH)
    loads[3].wait()
    query_pos = q_start[0] + lax.broadcasted_iota(jnp.int32, (slab, rows), 1)

    @pl.loop(0, shards)
    def _(slot):
        key_pos = starts[slot] + lax.broadcasted_iota(jnp.int32, (slab, rows), 0)
        bias[slot] = jnp.where(key_pos <= query_pos, 0.0, HIDDEN)

    for load in loads[:3]:
        load.wait()

    products = front(*order[0])
    ready = False
    for index, (turn, away) in enumerate(order):
        later = None
        if index + 1 < len(order):
            take(*order[index + 1])
            later = front(*order[index + 1])
        parts = back(turn, away, products)
        if away:
            hand_in(turn, away, *parts)
        else:
            if outer > 1 and not ready:
                pl.semaphore_wait(side_ready, outer - 1)
                ready = True
            pass_on(turn, *parts)
        products = later

    for head in range(KV_HEADS):
        keys = pairs[head, :, 0].reshape(total_keys, HEAD_DIM)
        for member in range(GROUP):
            query_head = head * GROUP + member
            columns = pl.ds(query_head * HEAD_DIM, HEAD_DIM)
            dq_all[:, columns] = contract(ds_all[query_head], keys, 0, 0) * SCALE

    all_arrived(starts, start_send, shards - reader - 1, range(1, shards))
    for turn in range(turns):
        all_arrived(pairs.at[0], pair_send.at[turn], shards - reader - 1, range(1, shards))
        for away in range(1, inner):
            arrived(pairs.at[0], hop_send.at[turn, away])
            arrived(part_out.at[0, 0], part_send.at[turn, away - 1])
        sent = seen - (owner_side(turn) == side).astype(jnp.int32)
        all_arrived(sum_out.at[turn], sum_send.at[turn], sent, range(1, shards + 1))

    for block in range(per_section):
        counts = range(2 * outer - 1, outer * shards, outer)
        all_arrived(sum_in.at[block], sum_recv.at[block], outer * (shards - reader) - 1, counts)
        columns = pl.ds(block * HEAD_DIM, HEAD_DIM)
        arrivals = sum_in[block].astype(jnp.float32)
        dk_out[:, columns] = jnp.sum(arrivals[:, 0], axis=0) * SCALE
        dv_out[:, columns] = jnp.sum(arrivals[:, 1], axis=0)


def write_out(dq_all, dk_all, dv_all, dq_hbm, dk_hbm, dv_hbm, sems):
    rows = dq_all.shape[0] // WRITES
    copies = [
        pltpu.make_async_copy(dk_all, dk_hbm, sems.at[WRITES]),
        pltpu.make_async_copy(dv_all, dv_hbm, sems.at[WRITES + 1]),
    ]
    for part in range(WRITES):
        span = pl.ds(part * rows, rows)
        copies.append(pltpu.make_async_copy(dq_all.at[span], dq_hbm.at[0, span], sems.at[part]))
    for copy in copies:
        copy.start()
    for copy in copies:
        copy.wait()


def per_device(
    sections, shards, queries, out_grads, logsumexp, shared_keys, shared_values, query_starts, slab_starts
):
    rows, width = queries.shape[1], queries.shape[2]
    slab, kv_width = shared_keys.shape
    heads = logsumexp.shape[1]
    inner = inner_factor(sections)
    outer = sections // inner
    turns = KV_HEADS // inner
    per_section = KV_HEADS // sections
    half, full = jnp.bfloat16, jnp.float32
    stack = (shards, 2, slab, HEAD_DIM)
    dma = pltpu.SemaphoreType.DMA
    hbm = pl.BlockSpec(memory_space=pl.ANY)
    vmem = pl.BlockSpec(memory_space=pltpu.VMEM)
    share = (slab, kv_width // sections)
    results = (((rows, width), full), (share, full), (share, full))
    grads = pl.pallas_call(
        functools.partial(kernel, sections, shards),
        out_shape=tuple(pltpu.VMEM(*result) for result in results),
        in_specs=[hbm] * 7,
        out_specs=(vmem, vmem, vmem),
        scratch_shapes=[
            pltpu.VMEM((rows, width), half),
            pltpu.VMEM((rows, width), half),
            pltpu.VMEM((heads, rows), full),
            pltpu.VMEM((KV_HEADS,) + stack, half),
            pltpu.VMEM((shards, 1, rows), jnp.int32),
            pltpu.VMEM((shards, slab, rows), full),
            pltpu.VMEM((heads, shards * slab, rows), half),
            pltpu.VMEM((turns, max(inner - 1, 1)) + stack, half),
            pltpu.VMEM((turns, max(inner - 1, 1)) + stack, half),
            pltpu.VMEM((turns,) + stack, half),
            pltpu.VMEM((per_section, outer * shards) + stack[1:], half),
            pltpu.SMEM((1,), jnp.int32),
            pltpu.SMEM((1,), jnp.int32),
            dma((5,)),
            dma,
            dma,
            dma,
            dma((turns,)),
            dma((turns,)),
            dma((turns, inner)),
            dma((turns, inner)),
            dma((turns, max(inner - 1, 1))),
            dma((turns, max(inner - 1, 1))),
            dma((turns,)),
            dma((per_section,)),
            pltpu.SemaphoreType.REGULAR,
        ],
        compiler_params=pltpu.CompilerParams(
            collective_id=0, has_side_effects=True, vmem_limit_bytes=56 * 2**20
        ),
    )(queries, out_grads, logsumexp, shared_keys, shared_values, query_starts, slab_starts)
    return pl.pallas_call(
        write_out,
        out_shape=(
            jax.ShapeDtypeStruct((1, rows, width), full),
            jax.ShapeDtypeStruct(share, full),
            jax.ShapeDtypeStruct(share, full),
        ),
        in_specs=[vmem, vmem, vmem],
        out_specs=(hbm, hbm, hbm),
        scratch_shapes=[dma((WRITES + 2,))],
    )(*(pltpu.with_memory_space_constraint(grad, pltpu.VMEM) for grad in grads))


def solution(mesh):
    return jax.shard_map(
        functools.partial(per_device, mesh.shape["section"], mesh.shape["seq"]),
        mesh=mesh,
        in_specs=(
            P("section", "seq", None),
            P("section", "seq", None),
            P("section", None, "seq"),
            P("seq", None),
            P("seq", None),
            P("seq"),
            P("seq"),
        ),
        out_specs=(P("section", "seq", None), P("seq", "section"), P("seq", "section")),
        check_vma=False,
    )
```

```python
import functools

import jax
import jax.numpy as jnp
from jax import lax
from jax.experimental import pallas as pl
from jax.experimental.pallas import tpu as pltpu
from jax.sharding import PartitionSpec as P

Q_HEADS = 24
KV_HEADS = 8
HEAD_DIM = 128
GROUP = Q_HEADS // KV_HEADS
SCALE = HEAD_DIM ** (-0.5)
LOG2E = 1.4426950408889634
HIDDEN = -1e30
FAR = 2**30
WRITES = 4
MESH = pl.DeviceIdType.MESH


def inner_factor(size):
    factor = 1
    while size % (2 * factor) == 0 and (2 * factor) ** 2 <= size:
        factor *= 2
    return factor


def contract(left, right, left_dim, right_dim):
    return lax.dot_general(
        left, right, (((left_dim,), (right_dim,)), ((), ())), preferred_element_type=jnp.float32
    )


def arrived(ref, sem):
    pltpu.make_async_copy(ref, ref, sem).wait()


def all_arrived(ref, sem, count, counts):
    for size in counts:

        @pl.when(count == size)
        def _():
            arrived(ref.at[pl.ds(0, size)], sem)


def order_of(inner, turns, early):
    order = [(turn, away) for turn in range(early) for away in range(1, inner)]
    order += [(turn, 0) for turn in range(early)]
    for turn in range(early, turns):
        order += [(turn, away) for away in [*range(1, inner), 0]]
    return order


def kernel(
    sections, shards, q_hbm, g_hbm, lse_hbm, k_hbm, v_hbm, q_start_hbm, k_start_hbm,
    dq_all, dk_out, dv_out,
    q_all, g_all, lse_all, pairs, starts, bias, ds_all, part_out, part_in, sum_out, sum_in, q_start, k_start,
    load_sem, pair_sem, start_send, start_recv, pair_send, pair_recv,
    hop_send, hop_recv, part_send, part_recv, sum_send, sum_recv, side_ready,
):
    inner = inner_factor(sections)
    outer = sections // inner
    turns = KV_HEADS // inner
    per_section = KV_HEADS // sections
    rows = q_all.shape[0]
    slab = pairs.shape[3]
    total_keys = shards * slab
    section, me = lax.axis_index("section"), lax.axis_index("seq")
    side, core = section // inner, lax.rem(section, inner)
    seen = jnp.minimum(me + 2, shards)
    reader = jnp.maximum(me - 1, 0)
    beside = jnp.minimum(me + 1, shards - 1) - reader

    def owner_side(turn):
        return turn // per_section

    def block_of(turn):
        return turn % per_section

    def head_of(turn, away):
        owner = owner_side(turn) * inner + lax.rem(core + away, inner)
        return owner * per_section + block_of(turn)

    def across(away):
        return (lax.rem(side + away, outer) * inner + core, me)

    def partner(away):
        return (side * inner + lax.rem(core + away, inner), me)

    first = 1 % inner
    barrier = pltpu.get_barrier_semaphore()

    @pl.loop(0, seen)
    def _(owner):
        @pl.when(owner != me)
        def _():
            pl.semaphore_signal(barrier, inc=1, device_id=(section, owner), device_id_type=MESH)

    for away in range(1, inner):
        pl.semaphore_signal(barrier, inc=1, device_id=partner(away), device_id_type=MESH)
    for away in range(1, outer):
        pl.semaphore_signal(barrier, inc=1, device_id=across(away), device_id_type=MESH)

    place_load = pltpu.make_async_copy(k_start_hbm, k_start, load_sem.at[4])
    place_load.start()
    for turn in range(turns):
        head = head_of(turn, first)
        columns = pl.ds(pl.multiple_of(head * HEAD_DIM, HEAD_DIM), HEAD_DIM)
        pltpu.make_async_copy(k_hbm.at[:, columns], pairs.at[head, me, 0], pair_sem).start()
        pltpu.make_async_copy(v_hbm.at[:, columns], pairs.at[head, me, 1], pair_sem).start()

    loads = [
        pltpu.make_async_copy(q_hbm.at[0], q_all, load_sem.at[0]),
        pltpu.make_async_copy(g_hbm.at[0], g_all, load_sem.at[1]),
        pltpu.make_async_copy(lse_hbm.at[0], lse_all, load_sem.at[2]),
        pltpu.make_async_copy(q_start_hbm, q_start, load_sem.at[3]),
    ]
    for load in loads:
        load.start()

    @pl.loop(seen, shards)
    def _(owner):
        starts[owner] = jnp.full((1, rows), FAR, jnp.int32)
        for turn in range(turns):
            pairs[head_of(turn, first), owner] = jnp.zeros(pairs.shape[2:], pairs.dtype)

    @pl.loop(0, reader)
    def _(source):
        starts[source] = jnp.full((1, rows), -FAR, jnp.int32)
        for block in range(per_section):
            for place in range(outer):
                sum_in[block, place * shards + source] = jnp.zeros(sum_in.shape[2:], sum_in.dtype)

    place_load.wait()
    starts[me] = jnp.full((1, rows), k_start[0], jnp.int32)
    mine = pairs.at[pl.ds(0, turns), 0]
    pltpu.make_async_copy(mine, mine, pair_sem).wait()
    pl.semaphore_wait(barrier, shards - reader - 1 + inner - 1 + outer - 1)

    def to_readers(send):
        @pl.loop(0, shards - reader)
        def _(turned):
            reading = shards - 1 - turned

            @pl.when(reading != me)
            def _():
                send(reading)

    for turn in range(turns):
        head = head_of(turn, first)
        if turn >= per_section:
            for done in range(turn) if turn == per_section else (turn - 1,):
                all_arrived(pairs.at[0], pair_send.at[done], shards - reader - 1, range(1, shards))

        @to_readers
        def _(reading):
            pltpu.make_async_remote_copy(
                src_ref=pairs.at[head, me],
                dst_ref=pairs.at[head, me],
                send_sem=pair_send.at[turn],
                recv_sem=pair_recv.at[turn],
                device_id=(section, reading),
                device_id_type=MESH,
            ).start()

        if turn == 0:
            for near in (1, -1):
                @pl.when((me + near >= 0) & (me + near < shards))
                def _():
                    pltpu.make_async_remote_copy(
                        src_ref=starts.at[me],
                        dst_ref=starts.at[me],
                        send_sem=start_send,
                        recv_sem=start_recv,
                        device_id=(section, me + near),
                        device_id_type=MESH,
                    ).start()

    def take(turn, away):
        head = head_of(turn, away)
        if away != first:
            arrived(pairs.at[head], hop_recv.at[turn, away])
            return

        all_arrived(pairs.at[head], pair_recv.at[turn], seen - 1, range(1, shards))

        for forward in range(1, inner):
            pltpu.make_async_remote_copy(
                src_ref=pairs.at[head],
                dst_ref=pairs.at[head],
                send_sem=hop_send.at[turn, forward],
                recv_sem=hop_recv.at[turn, (first - forward) % inner],
                device_id=partner(forward),
                device_id_type=MESH,
            ).start()

    def columns_of(query_head):
        return pl.ds(pl.multiple_of(query_head * HEAD_DIM, HEAD_DIM), HEAD_DIM)

    def front(turn, away):
        head = head_of(turn, away)
        keys = pairs[head, :, 0].reshape(total_keys, HEAD_DIM)
        values = pairs[head, :, 1].reshape(total_keys, HEAD_DIM)
        products = []
        for member in range(GROUP):
            columns = columns_of(head * GROUP + member)
            products.append((contract(keys, q_all[:, columns], 1, 1), contract(values, g_all[:, columns], 1, 1)))
        return products

    def back(turn, away, products):
        head = head_of(turn, away)
        hidden = bias[...].reshape(total_keys, rows)
        all_probs, all_scores, queries, grads = [], [], [], []
        for member in range(GROUP):
            query_head = head * GROUP + member
            scores, grad_probs = products[member]
            probs = jnp.exp2(scores * (SCALE * LOG2E) + (hidden - lse_all[pl.ds(query_head, 1), :] * LOG2E))
            delta = jnp.sum(probs * grad_probs, axis=0, keepdims=True)
            scores_half = (probs * (grad_probs - delta)).astype(jnp.bfloat16)
            ds_all[query_head] = scores_half
            all_probs.append(probs.astype(jnp.bfloat16))
            all_scores.append(scores_half)
            queries.append(q_all[:, columns_of(query_head)])
            grads.append(g_all[:, columns_of(query_head)])
        key_part = contract(jnp.concatenate(all_scores, 1), jnp.concatenate(queries, 0), 1, 0)
        value_part = contract(jnp.concatenate(all_probs, 1), jnp.concatenate(grads, 0), 1, 0)
        return key_part.reshape(shards, slab, HEAD_DIM), value_part.reshape(shards, slab, HEAD_DIM)

    def hand_in(turn, away, key_part, value_part):
        part_out[turn, away - 1, :, 0] = key_part.astype(jnp.bfloat16)
        part_out[turn, away - 1, :, 1] = value_part.astype(jnp.bfloat16)
        pltpu.make_async_remote_copy(
            src_ref=part_out.at[turn, away - 1],
            dst_ref=part_in.at[turn, away - 1],
            send_sem=part_send.at[turn, away - 1],
            recv_sem=part_recv.at[turn, away - 1],
            device_id=partner(away),
            device_id_type=MESH,
        ).start()

    def pass_on(turn, key_part, value_part):
        for away in range(1, inner):
            arrived(part_in.at[turn, away - 1], part_recv.at[turn, away - 1])
            key_part = key_part + part_in[turn, away - 1, :, 0].astype(jnp.float32)
            value_part = value_part + part_in[turn, away - 1, :, 1].astype(jnp.float32)
        sum_out[turn, :, 0] = key_part.astype(jnp.bfloat16)
        sum_out[turn, :, 1] = value_part.astype(jnp.bfloat16)
        target = owner_side(turn)
        block = block_of(turn)

        for owner in range(shards):
            @pl.when(((owner != me) | (target != side)) & (owner < seen))
            def _():
                pltpu.make_async_remote_copy(
                    src_ref=sum_out.at[turn, owner],
                    dst_ref=sum_in.at[block, side * shards + me],
                    send_sem=sum_send.at[turn],
                    recv_sem=sum_recv.at[block],
                    device_id=(target * inner + core, owner),
                    device_id_type=MESH,
                ).start()

        @pl.when(target == side)
        def _():
            sum_in[block, side * shards + me] = sum_out[turn, me]

    order = order_of(inner, turns, per_section)
    take(*order[0])

    all_arrived(starts, start_recv, beside, range(1, 3))

    for away in range(1, outer):
        pl.semaphore_signal(side_ready, inc=1, device_id=across(away), device_id_type=MESH)
    loads[3].wait()
    query_pos = q_start[0] + lax.broadcasted_iota(jnp.int32, (slab, rows), 1)

    @pl.loop(0, shards)
    def _(slot):
        key_pos = starts[slot] + lax.broadcasted_iota(jnp.int32, (slab, rows), 0)
        bias[slot] = jnp.where(key_pos <= query_pos, 0.0, HIDDEN)

    for load in loads[:3]:
        load.wait()

    ready = outer == 1
    for index, (turn, away) in enumerate(order):
        if index:
            take(turn, away)
        parts = back(turn, away, front(turn, away))
        if away:
            hand_in(turn, away, *parts)
            continue
        if not ready:
            pl.semaphore_wait(side_ready, outer - 1)
            ready = True
        pass_on(turn, *parts)

    for head in range(KV_HEADS):
        keys = pairs[head, :, 0].reshape(total_keys, HEAD_DIM)
        for member in range(GROUP):
            query_head = head * GROUP + member
            columns = pl.ds(query_head * HEAD_DIM, HEAD_DIM)
            dq_all[:, columns] = contract(ds_all[query_head], keys, 0, 0) * SCALE

    all_arrived(starts, start_send, beside, range(1, 3))
    for turn in range(turns):
        if turn == turns - 1 or outer == 1:
            all_arrived(pairs.at[0], pair_send.at[turn], shards - reader - 1, range(1, shards))
        for away in range(1, inner):
            arrived(pairs.at[0], hop_send.at[turn, away])
            arrived(part_out.at[0, 0], part_send.at[turn, away - 1])
        sent = seen - (owner_side(turn) == side).astype(jnp.int32)
        all_arrived(sum_out.at[turn], sum_send.at[turn], sent, range(1, shards + 1))

    for block in range(per_section):
        counts = range(2 * outer - 1, outer * shards, outer)
        all_arrived(sum_in.at[block], sum_recv.at[block], outer * (shards - reader) - 1, counts)
        columns = pl.ds(block * HEAD_DIM, HEAD_DIM)
        arrivals = sum_in[block].astype(jnp.float32)
        dk_out[:, columns] = jnp.sum(arrivals[:, 0], axis=0) * SCALE
        dv_out[:, columns] = jnp.sum(arrivals[:, 1], axis=0)


def write_out(dq_all, dk_all, dv_all, dq_hbm, dk_hbm, dv_hbm, sems):
    rows = dq_all.shape[0] // WRITES
    copies = [
        pltpu.make_async_copy(dk_all, dk_hbm, sems.at[WRITES]),
        pltpu.make_async_copy(dv_all, dv_hbm, sems.at[WRITES + 1]),
    ]
    for part in range(WRITES):
        span = pl.ds(part * rows, rows)
        copies.append(pltpu.make_async_copy(dq_all.at[span], dq_hbm.at[0, span], sems.at[part]))
    for copy in copies:
        copy.start()
    for copy in copies:
        copy.wait()


def per_device(
    sections, shards, queries, out_grads, logsumexp, shared_keys, shared_values, query_starts, slab_starts
):
    rows, width = queries.shape[1], queries.shape[2]
    slab, kv_width = shared_keys.shape
    heads = logsumexp.shape[1]
    inner = inner_factor(sections)
    outer = sections // inner
    turns = KV_HEADS // inner
    per_section = KV_HEADS // sections
    half, full = jnp.bfloat16, jnp.float32
    stack = (shards, 2, slab, HEAD_DIM)
    dma = pltpu.SemaphoreType.DMA
    hbm = pl.BlockSpec(memory_space=pl.ANY)
    vmem = pl.BlockSpec(memory_space=pltpu.VMEM)
    share = (slab, kv_width // sections)
    results = (((rows, width), full), (share, full), (share, full))
    grads = pl.pallas_call(
        functools.partial(kernel, sections, shards),
        out_shape=tuple(pltpu.VMEM(*result) for result in results),
        in_specs=[hbm] * 7,
        out_specs=(vmem, vmem, vmem),
        scratch_shapes=[
            pltpu.VMEM((rows, width), half),
            pltpu.VMEM((rows, width), half),
            pltpu.VMEM((heads, rows), full),
            pltpu.VMEM((KV_HEADS,) + stack, half),
            pltpu.VMEM((shards, 1, rows), jnp.int32),
            pltpu.VMEM((shards, slab, rows), full),
            pltpu.VMEM((heads, shards * slab, rows), half),
            pltpu.VMEM((turns, max(inner - 1, 1)) + stack, half),
            pltpu.VMEM((turns, max(inner - 1, 1)) + stack, half),
            pltpu.VMEM((turns,) + stack, half),
            pltpu.VMEM((per_section, outer * shards) + stack[1:], half),
            pltpu.SMEM((1,), jnp.int32),
            pltpu.SMEM((1,), jnp.int32),
            dma((5,)),
            dma,
            dma,
            dma,
            dma((turns,)),
            dma((turns,)),
            dma((turns, inner)),
            dma((turns, inner)),
            dma((turns, max(inner - 1, 1))),
            dma((turns, max(inner - 1, 1))),
            dma((turns,)),
            dma((per_section,)),
            pltpu.SemaphoreType.REGULAR,
        ],
        compiler_params=pltpu.CompilerParams(
            collective_id=0, has_side_effects=True, vmem_limit_bytes=56 * 2**20
        ),
    )(queries, out_grads, logsumexp, shared_keys, shared_values, query_starts, slab_starts)
    return pl.pallas_call(
        write_out,
        out_shape=(
            jax.ShapeDtypeStruct((1, rows, width), full),
            jax.ShapeDtypeStruct(share, full),
            jax.ShapeDtypeStruct(share, full),
        ),
        in_specs=[vmem, vmem, vmem],
        out_specs=(hbm, hbm, hbm),
        scratch_shapes=[dma((WRITES + 2,))],
    )(*(pltpu.with_memory_space_constraint(grad, pltpu.VMEM) for grad in grads))


def solution(mesh):
    return jax.shard_map(
        functools.partial(per_device, mesh.shape["section"], mesh.shape["seq"]),
        mesh=mesh,
        in_specs=(
            P("section", "seq", None),
            P("section", "seq", None),
            P("section", None, "seq"),
            P("seq", None),
            P("seq", None),
            P("seq"),
            P("seq"),
        ),
        out_specs=(P("section", "seq", None), P("seq", "section"), P("seq", "section")),
        check_vma=False,
    )
```

```python
import functools

import jax
import jax.numpy as jnp
from jax import lax
from jax.experimental import pallas as pl
from jax.experimental.pallas import tpu as pltpu
from jax.sharding import PartitionSpec as P

Q_HEADS = 24
KV_HEADS = 8
HEAD_DIM = 128
GROUP = Q_HEADS // KV_HEADS
SCALE = HEAD_DIM ** (-0.5)
LOG2E = 1.4426950408889634
HIDDEN = -1e30
FAR = 2**30
WRITES = 4
MESH = pl.DeviceIdType.MESH


def inner_factor(size):
    factor = 1
    while size % (2 * factor) == 0 and (2 * factor) ** 2 <= size:
        factor *= 2
    return factor


def contract(left, right, left_dim, right_dim):
    return lax.dot_general(
        left, right, (((left_dim,), (right_dim,)), ((), ())), preferred_element_type=jnp.float32
    )


def arrived(ref, sem):
    pltpu.make_async_copy(ref, ref, sem).wait()


def all_arrived(ref, sem, count, counts):
    for size in counts:

        @pl.when(count == size)
        def _():
            arrived(ref.at[pl.ds(0, size)], sem)


def order_of(inner, turns, early):
    order = [(turn, away) for turn in range(early) for away in range(1, inner)]
    order += [(turn, 0) for turn in range(early)]
    for turn in range(early, turns):
        order += [(turn, away) for away in [*range(1, inner), 0]]
    return order


def kernel(
    sections, shards, q_hbm, g_hbm, lse_hbm, k_hbm, v_hbm, q_start_hbm, k_start_hbm,
    dq_all, dk_out, dv_out,
    q_all, g_all, lse_all, pairs, starts, bias, ds_all, part_out, part_in, sum_out, sum_in, q_start, k_start,
    load_sem, pair_sem, start_send, start_recv, pair_send, pair_recv,
    hop_send, hop_recv, part_send, part_recv, sum_send, sum_recv, side_ready,
):
    inner = inner_factor(sections)
    outer = sections // inner
    turns = KV_HEADS // inner
    per_section = KV_HEADS // sections
    rows = q_all.shape[0]
    slab = pairs.shape[3]
    total_keys = shards * slab
    section, me = lax.axis_index("section"), lax.axis_index("seq")
    side, core = section // inner, lax.rem(section, inner)
    seen = jnp.minimum(me + 2, shards)
    reader = jnp.maximum(me - 1, 0)
    beside = jnp.minimum(me + 1, shards - 1) - reader

    def owner_side(turn):
        return turn // per_section

    def block_of(turn):
        return turn % per_section

    def head_of(turn, away):
        owner = owner_side(turn) * inner + lax.rem(core + away, inner)
        return owner * per_section + block_of(turn)

    def across(away):
        return (lax.rem(side + away, outer) * inner + core, me)

    def partner(away):
        return (side * inner + lax.rem(core + away, inner), me)

    first = 1 % inner
    barrier = pltpu.get_barrier_semaphore()

    @pl.loop(0, seen)
    def _(owner):
        @pl.when(owner != me)
        def _():
            pl.semaphore_signal(barrier, inc=1, device_id=(section, owner), device_id_type=MESH)

    for away in range(1, inner):
        pl.semaphore_signal(barrier, inc=1, device_id=partner(away), device_id_type=MESH)
    for away in range(1, outer):
        pl.semaphore_signal(barrier, inc=1, device_id=across(away), device_id_type=MESH)

    place_load = pltpu.make_async_copy(k_start_hbm, k_start, load_sem.at[4])
    place_load.start()
    for turn in range(turns):
        head = head_of(turn, first)
        columns = pl.ds(pl.multiple_of(head * HEAD_DIM, HEAD_DIM), HEAD_DIM)
        pltpu.make_async_copy(k_hbm.at[:, columns], pairs.at[head, me, 0], pair_sem).start()
        pltpu.make_async_copy(v_hbm.at[:, columns], pairs.at[head, me, 1], pair_sem).start()

    loads = [
        pltpu.make_async_copy(q_hbm.at[0], q_all, load_sem.at[0]),
        pltpu.make_async_copy(g_hbm.at[0], g_all, load_sem.at[1]),
        pltpu.make_async_copy(lse_hbm.at[0], lse_all, load_sem.at[2]),
        pltpu.make_async_copy(q_start_hbm, q_start, load_sem.at[3]),
    ]
    for load in loads:
        load.start()

    @pl.loop(seen, shards)
    def _(owner):
        starts[owner] = jnp.full((1, rows), FAR, jnp.int32)
        for turn in range(turns):
            pairs[head_of(turn, first), owner] = jnp.zeros(pairs.shape[2:], pairs.dtype)

    @pl.loop(0, reader)
    def _(source):
        starts[source] = jnp.full((1, rows), -FAR, jnp.int32)
        for block in range(per_section):
            for place in range(outer):
                sum_in[block, place * shards + source] = jnp.zeros(sum_in.shape[2:], sum_in.dtype)

    place_load.wait()
    starts[me] = jnp.full((1, rows), k_start[0], jnp.int32)
    mine = pairs.at[pl.ds(0, turns), 0]
    pltpu.make_async_copy(mine, mine, pair_sem).wait()
    pl.semaphore_wait(barrier, shards - reader - 1 + inner - 1 + outer - 1)

    def to_readers(send):
        @pl.loop(0, shards - reader)
        def _(turned):
            reading = shards - 1 - turned

            @pl.when(reading != me)
            def _():
                send(reading)

    def landed(turn):
        all_arrived(pairs.at[0], pair_send.at[turn], shards - reader - 1, range(1, shards))

    def send(turn):
        head = head_of(turn, first)

        @to_readers
        def _(reading):
            pltpu.make_async_remote_copy(
                src_ref=pairs.at[head, me],
                dst_ref=pairs.at[head, me],
                send_sem=pair_send.at[turn],
                recv_sem=pair_recv.at[turn],
                device_id=(section, reading),
                device_id_type=MESH,
            ).start()

    early = range(per_section)
    later = range(per_section, turns)
    send(0)
    for near in (1, -1):
        @pl.when((me + near >= 0) & (me + near < shards))
        def _():
            pltpu.make_async_remote_copy(
                src_ref=starts.at[me],
                dst_ref=starts.at[me],
                send_sem=start_send,
                recv_sem=start_recv,
                device_id=(section, me + near),
                device_id_type=MESH,
            ).start()

    for turn in early[1:]:
        send(turn)

    many = me < shards * 3 // 4

    @pl.when(many)
    def _():
        for turn in later:
            for done in early if turn == later[0] else (turn - 1,):
                landed(done)
            send(turn)

    @pl.when(jnp.logical_not(many))
    def _():
        for turn in later:
            send(turn)

    def take(turn, away):
        head = head_of(turn, away)
        if away != first:
            arrived(pairs.at[head], hop_recv.at[turn, away])
            return

        all_arrived(pairs.at[head], pair_recv.at[turn], seen - 1, range(1, shards))

        for forward in range(1, inner):
            pltpu.make_async_remote_copy(
                src_ref=pairs.at[head],
                dst_ref=pairs.at[head],
                send_sem=hop_send.at[turn, forward],
                recv_sem=hop_recv.at[turn, (first - forward) % inner],
                device_id=partner(forward),
                device_id_type=MESH,
            ).start()

    def columns_of(query_head):
        return pl.ds(pl.multiple_of(query_head * HEAD_DIM, HEAD_DIM), HEAD_DIM)

    def front(turn, away):
        head = head_of(turn, away)
        keys = pairs[head, :, 0].reshape(total_keys, HEAD_DIM)
        values = pairs[head, :, 1].reshape(total_keys, HEAD_DIM)
        products = []
        for member in range(GROUP):
            columns = columns_of(head * GROUP + member)
            products.append((contract(keys, q_all[:, columns], 1, 1), contract(values, g_all[:, columns], 1, 1)))
        return products

    def back(turn, away, products):
        head = head_of(turn, away)
        key_part = jnp.zeros((total_keys, HEAD_DIM), jnp.float32)
        value_part = jnp.zeros((total_keys, HEAD_DIM), jnp.float32)
        hidden = bias[...].reshape(total_keys, rows)
        for member in range(GROUP):
            query_head = head * GROUP + member
            scores, grad_probs = products[member]
            probs = jnp.exp2(scores * (SCALE * LOG2E) + (hidden - lse_all[pl.ds(query_head, 1), :] * LOG2E))
            delta = jnp.sum(probs * grad_probs, axis=0, keepdims=True)
            scores_half = (probs * (grad_probs - delta)).astype(jnp.bfloat16)
            ds_all[query_head] = scores_half
            value_part += contract(probs.astype(jnp.bfloat16), g_all[:, columns_of(query_head)], 1, 0)
            key_part += contract(scores_half, q_all[:, columns_of(query_head)], 1, 0)
        return key_part.reshape(shards, slab, HEAD_DIM), value_part.reshape(shards, slab, HEAD_DIM)

    def hand_in(turn, away, key_part, value_part):
        part_out[turn, away - 1, :, 0] = key_part.astype(jnp.bfloat16)
        part_out[turn, away - 1, :, 1] = value_part.astype(jnp.bfloat16)
        pltpu.make_async_remote_copy(
            src_ref=part_out.at[turn, away - 1],
            dst_ref=part_in.at[turn, away - 1],
            send_sem=part_send.at[turn, away - 1],
            recv_sem=part_recv.at[turn, away - 1],
            device_id=partner(away),
            device_id_type=MESH,
        ).start()

    def pass_on(turn, key_part, value_part):
        for away in range(1, inner):
            arrived(part_in.at[turn, away - 1], part_recv.at[turn, away - 1])
            key_part = key_part + part_in[turn, away - 1, :, 0].astype(jnp.float32)
            value_part = value_part + part_in[turn, away - 1, :, 1].astype(jnp.float32)
        sum_out[turn, :, 0] = key_part.astype(jnp.bfloat16)
        sum_out[turn, :, 1] = value_part.astype(jnp.bfloat16)
        target = owner_side(turn)
        block = block_of(turn)

        for owner in range(shards):
            @pl.when(((owner != me) | (target != side)) & (owner < seen))
            def _():
                pltpu.make_async_remote_copy(
                    src_ref=sum_out.at[turn, owner],
                    dst_ref=sum_in.at[block, side * shards + me],
                    send_sem=sum_send.at[turn],
                    recv_sem=sum_recv.at[block],
                    device_id=(target * inner + core, owner),
                    device_id_type=MESH,
                ).start()

        @pl.when(target == side)
        def _():
            sum_in[block, side * shards + me] = sum_out[turn, me]

    order = order_of(inner, turns, per_section)
    take(*order[0])

    all_arrived(starts, start_recv, beside, range(1, 3))

    for away in range(1, outer):
        pl.semaphore_signal(side_ready, inc=1, device_id=across(away), device_id_type=MESH)
    loads[3].wait()
    query_pos = q_start[0] + lax.broadcasted_iota(jnp.int32, (slab, rows), 1)

    @pl.loop(0, shards)
    def _(slot):
        key_pos = starts[slot] + lax.broadcasted_iota(jnp.int32, (slab, rows), 0)
        bias[slot] = jnp.where(key_pos <= query_pos, 0.0, HIDDEN)

    for load in loads[:3]:
        load.wait()

    ready = outer == 1
    for index, (turn, away) in enumerate(order):
        if index:
            take(turn, away)
        parts = back(turn, away, front(turn, away))
        if away:
            hand_in(turn, away, *parts)
            continue
        if not ready:
            pl.semaphore_wait(side_ready, outer - 1)
            ready = True
        pass_on(turn, *parts)

    for head in range(KV_HEADS):
        keys = pairs[head, :, 0].reshape(total_keys, HEAD_DIM)
        for member in range(GROUP):
            query_head = head * GROUP + member
            columns = pl.ds(query_head * HEAD_DIM, HEAD_DIM)
            dq_all[:, columns] = contract(ds_all[query_head], keys, 0, 0) * SCALE

    all_arrived(starts, start_send, beside, range(1, 3))
    for turn in range(turns):
        if turn == turns - 1 or not later:
            landed(turn)
        else:
            @pl.when(jnp.logical_not(many))
            def _():
                landed(turn)

    for turn in range(turns):
        for away in range(1, inner):
            arrived(pairs.at[0], hop_send.at[turn, away])
            arrived(part_out.at[0, 0], part_send.at[turn, away - 1])
        sent = seen - (owner_side(turn) == side).astype(jnp.int32)
        all_arrived(sum_out.at[turn], sum_send.at[turn], sent, range(1, shards + 1))

    for block in range(per_section):
        counts = range(2 * outer - 1, outer * shards, outer)
        all_arrived(sum_in.at[block], sum_recv.at[block], outer * (shards - reader) - 1, counts)
        columns = pl.ds(block * HEAD_DIM, HEAD_DIM)
        arrivals = sum_in[block].astype(jnp.float32)
        dk_out[:, columns] = jnp.sum(arrivals[:, 0], axis=0) * SCALE
        dv_out[:, columns] = jnp.sum(arrivals[:, 1], axis=0)


def write_out(dq_all, dk_all, dv_all, dq_hbm, dk_hbm, dv_hbm, sems):
    rows = dq_all.shape[0] // WRITES
    copies = [
        pltpu.make_async_copy(dk_all, dk_hbm, sems.at[WRITES]),
        pltpu.make_async_copy(dv_all, dv_hbm, sems.at[WRITES + 1]),
    ]
    for part in range(WRITES):
        span = pl.ds(part * rows, rows)
        copies.append(pltpu.make_async_copy(dq_all.at[span], dq_hbm.at[0, span], sems.at[part]))
    for copy in copies:
        copy.start()
    for copy in copies:
        copy.wait()


def per_device(
    sections, shards, queries, out_grads, logsumexp, shared_keys, shared_values, query_starts, slab_starts
):
    rows, width = queries.shape[1], queries.shape[2]
    slab, kv_width = shared_keys.shape
    heads = logsumexp.shape[1]
    inner = inner_factor(sections)
    outer = sections // inner
    turns = KV_HEADS // inner
    per_section = KV_HEADS // sections
    half, full = jnp.bfloat16, jnp.float32
    stack = (shards, 2, slab, HEAD_DIM)
    dma = pltpu.SemaphoreType.DMA
    hbm = pl.BlockSpec(memory_space=pl.ANY)
    vmem = pl.BlockSpec(memory_space=pltpu.VMEM)
    share = (slab, kv_width // sections)
    results = (((rows, width), full), (share, full), (share, full))
    grads = pl.pallas_call(
        functools.partial(kernel, sections, shards),
        out_shape=tuple(pltpu.VMEM(*result) for result in results),
        in_specs=[hbm] * 7,
        out_specs=(vmem, vmem, vmem),
        scratch_shapes=[
            pltpu.VMEM((rows, width), half),
            pltpu.VMEM((rows, width), half),
            pltpu.VMEM((heads, rows), full),
            pltpu.VMEM((KV_HEADS,) + stack, half),
            pltpu.VMEM((shards, 1, rows), jnp.int32),
            pltpu.VMEM((shards, slab, rows), full),
            pltpu.VMEM((heads, shards * slab, rows), half),
            pltpu.VMEM((turns, max(inner - 1, 1)) + stack, half),
            pltpu.VMEM((turns, max(inner - 1, 1)) + stack, half),
            pltpu.VMEM((turns,) + stack, half),
            pltpu.VMEM((per_section, outer * shards) + stack[1:], half),
            pltpu.SMEM((1,), jnp.int32),
            pltpu.SMEM((1,), jnp.int32),
            dma((5,)),
            dma,
            dma,
            dma,
            dma((turns,)),
            dma((turns,)),
            dma((turns, inner)),
            dma((turns, inner)),
            dma((turns, max(inner - 1, 1))),
            dma((turns, max(inner - 1, 1))),
            dma((turns,)),
            dma((per_section,)),
            pltpu.SemaphoreType.REGULAR,
        ],
        compiler_params=pltpu.CompilerParams(
            collective_id=0, has_side_effects=True, vmem_limit_bytes=56 * 2**20
        ),
    )(queries, out_grads, logsumexp, shared_keys, shared_values, query_starts, slab_starts)
    return pl.pallas_call(
        write_out,
        out_shape=(
            jax.ShapeDtypeStruct((1, rows, width), full),
            jax.ShapeDtypeStruct(share, full),
            jax.ShapeDtypeStruct(share, full),
        ),
        in_specs=[vmem, vmem, vmem],
        out_specs=(hbm, hbm, hbm),
        scratch_shapes=[dma((WRITES + 2,))],
    )(*(pltpu.with_memory_space_constraint(grad, pltpu.VMEM) for grad in grads))


def solution(mesh):
    return jax.shard_map(
        functools.partial(per_device, mesh.shape["section"], mesh.shape["seq"]),
        mesh=mesh,
        in_specs=(
            P("section", "seq", None),
            P("section", "seq", None),
            P("section", None, "seq"),
            P("seq", None),
            P("seq", None),
            P("seq"),
            P("seq"),
        ),
        out_specs=(P("section", "seq", None), P("seq", "section"), P("seq", "section")),
        check_vma=False,
    )
```

```python
import functools

import jax
import jax.numpy as jnp
from jax import lax
from jax.experimental import pallas as pl
from jax.experimental.pallas import tpu as pltpu
from jax.sharding import PartitionSpec as P

Q_HEADS = 24
KV_HEADS = 8
HEAD_DIM = 128
GROUP = Q_HEADS // KV_HEADS
SCALE = HEAD_DIM ** (-0.5)
LOG2E = 1.4426950408889634
HIDDEN = -1e30
FAR = 2**30
WRITES = 4
MESH = pl.DeviceIdType.MESH


def inner_factor(size):
    factor = 1
    while size % (2 * factor) == 0 and (2 * factor) ** 2 <= size:
        factor *= 2
    return factor


def contract(left, right, left_dim, right_dim):
    return lax.dot_general(
        left, right, (((left_dim,), (right_dim,)), ((), ())), preferred_element_type=jnp.float32
    )


def arrived(ref, sem):
    pltpu.make_async_copy(ref, ref, sem).wait()


def all_arrived(ref, sem, count, counts):
    for size in counts:

        @pl.when(count == size)
        def _():
            arrived(ref.at[pl.ds(0, size)], sem)


def order_of(inner, turns, early):
    order = [(turn, away) for turn in range(early) for away in range(1, inner)]
    order += [(turn, 0) for turn in range(early)]
    for turn in range(early, turns):
        order += [(turn, away) for away in [*range(1, inner), 0]]
    return order


def kernel(
    sections, shards, q_hbm, g_hbm, lse_hbm, k_hbm, v_hbm, q_start_hbm, k_start_hbm,
    dq_all, dk_out, dv_out,
    q_all, g_all, lse_all, pairs, starts, bias, ds_all, part_out, part_in, sum_out, sum_in, q_start, k_start,
    load_sem, pair_sem, start_send, start_recv, pair_send, pair_recv,
    hop_send, hop_recv, part_send, part_recv, sum_send, sum_recv, side_ready,
):
    inner = inner_factor(sections)
    outer = sections // inner
    turns = KV_HEADS // inner
    per_section = KV_HEADS // sections
    rows = q_all.shape[0]
    slab = pairs.shape[3]
    total_keys = shards * slab
    section, me = lax.axis_index("section"), lax.axis_index("seq")
    side, core = section // inner, lax.rem(section, inner)
    seen = jnp.minimum(me + 2, shards)
    reader = jnp.maximum(me - 1, 0)
    beside = jnp.minimum(me + 1, shards - 1) - reader

    def owner_side(turn):
        return turn // per_section

    def block_of(turn):
        return turn % per_section

    def head_of(turn, away):
        owner = owner_side(turn) * inner + lax.rem(core + away, inner)
        return owner * per_section + block_of(turn)

    def across(away):
        return (lax.rem(side + away, outer) * inner + core, me)

    def partner(away):
        return (side * inner + lax.rem(core + away, inner), me)

    first = 1 % inner
    barrier = pltpu.get_barrier_semaphore()

    @pl.loop(0, seen)
    def _(owner):
        @pl.when(owner != me)
        def _():
            pl.semaphore_signal(barrier, inc=1, device_id=(section, owner), device_id_type=MESH)

    for away in range(1, inner):
        pl.semaphore_signal(barrier, inc=1, device_id=partner(away), device_id_type=MESH)
    for away in range(1, outer):
        pl.semaphore_signal(barrier, inc=1, device_id=across(away), device_id_type=MESH)

    place_load = pltpu.make_async_copy(k_start_hbm, k_start, load_sem.at[4])
    place_load.start()
    for turn in range(turns):
        head = head_of(turn, first)
        columns = pl.ds(pl.multiple_of(head * HEAD_DIM, HEAD_DIM), HEAD_DIM)
        pltpu.make_async_copy(k_hbm.at[:, columns], pairs.at[head, me, 0], pair_sem).start()
        pltpu.make_async_copy(v_hbm.at[:, columns], pairs.at[head, me, 1], pair_sem).start()

    loads = [
        pltpu.make_async_copy(q_hbm.at[0], q_all, load_sem.at[0]),
        pltpu.make_async_copy(g_hbm.at[0], g_all, load_sem.at[1]),
        pltpu.make_async_copy(lse_hbm.at[0], lse_all, load_sem.at[2]),
        pltpu.make_async_copy(q_start_hbm, q_start, load_sem.at[3]),
    ]
    for load in loads:
        load.start()

    @pl.loop(seen, shards)
    def _(owner):
        starts[owner] = jnp.full((1, rows), FAR, jnp.int32)
        for turn in range(turns):
            pairs[head_of(turn, first), owner] = jnp.zeros(pairs.shape[2:], pairs.dtype)

    @pl.loop(0, reader)
    def _(source):
        starts[source] = jnp.full((1, rows), -FAR, jnp.int32)
        for block in range(per_section):
            for place in range(outer):
                sum_in[block, place * shards + source] = jnp.zeros(sum_in.shape[2:], sum_in.dtype)

    place_load.wait()
    starts[me] = jnp.full((1, rows), k_start[0], jnp.int32)
    mine = pairs.at[pl.ds(0, turns), 0]
    pltpu.make_async_copy(mine, mine, pair_sem).wait()
    pl.semaphore_wait(barrier, shards - reader - 1 + inner - 1 + outer - 1)

    def to_readers(send):
        @pl.loop(0, shards - reader)
        def _(turned):
            reading = shards - 1 - turned

            @pl.when(reading != me)
            def _():
                send(reading)

    for turn in range(turns):
        head = head_of(turn, first)
        if turn >= per_section:
            for done in range(turn) if turn == per_section else (turn - 1,):
                all_arrived(pairs.at[0], pair_send.at[done], shards - reader - 1, range(1, shards))

        @to_readers
        def _(reading):
            pltpu.make_async_remote_copy(
                src_ref=pairs.at[head, me],
                dst_ref=pairs.at[head, me],
                send_sem=pair_send.at[turn],
                recv_sem=pair_recv.at[turn],
                device_id=(section, reading),
                device_id_type=MESH,
            ).start()

        if turn == per_section - 1:
            for near in (1, -1):
                @pl.when((me + near >= 0) & (me + near < shards))
                def _():
                    pltpu.make_async_remote_copy(
                        src_ref=starts.at[me],
                        dst_ref=starts.at[me],
                        send_sem=start_send,
                        recv_sem=start_recv,
                        device_id=(section, me + near),
                        device_id_type=MESH,
                    ).start()

    def take(turn, away):
        head = head_of(turn, away)
        if away != first:
            arrived(pairs.at[head], hop_recv.at[turn, away])
            return

        all_arrived(pairs.at[head], pair_recv.at[turn], seen - 1, range(1, shards))

        for forward in range(1, inner):
            pltpu.make_async_remote_copy(
                src_ref=pairs.at[head],
                dst_ref=pairs.at[head],
                send_sem=hop_send.at[turn, forward],
                recv_sem=hop_recv.at[turn, (first - forward) % inner],
                device_id=partner(forward),
                device_id_type=MESH,
            ).start()

    def columns_of(query_head):
        return pl.ds(pl.multiple_of(query_head * HEAD_DIM, HEAD_DIM), HEAD_DIM)

    def front(turn, away):
        head = head_of(turn, away)
        keys = pairs[head, :, 0].reshape(total_keys, HEAD_DIM)
        values = pairs[head, :, 1].reshape(total_keys, HEAD_DIM)
        products = []
        for member in range(GROUP):
            columns = columns_of(head * GROUP + member)
            products.append((contract(keys, q_all[:, columns], 1, 1), contract(values, g_all[:, columns], 1, 1)))
        return products

    def back(turn, away, products):
        head = head_of(turn, away)
        key_part = jnp.zeros((total_keys, HEAD_DIM), jnp.float32)
        value_part = jnp.zeros((total_keys, HEAD_DIM), jnp.float32)
        hidden = bias[...].reshape(total_keys, rows)
        for member in range(GROUP):
            query_head = head * GROUP + member
            scores, grad_probs = products[member]
            probs = jnp.exp2(scores * (SCALE * LOG2E) + (hidden - lse_all[pl.ds(query_head, 1), :] * LOG2E))
            delta = jnp.sum(probs * grad_probs, axis=0, keepdims=True)
            scores_half = (probs * (grad_probs - delta)).astype(jnp.bfloat16)
            ds_all[query_head] = scores_half
            value_part += contract(probs.astype(jnp.bfloat16), g_all[:, columns_of(query_head)], 1, 0)
            key_part += contract(scores_half, q_all[:, columns_of(query_head)], 1, 0)
        return key_part.reshape(shards, slab, HEAD_DIM), value_part.reshape(shards, slab, HEAD_DIM)

    def hand_in(turn, away, key_part, value_part):
        part_out[turn, away - 1, :, 0] = key_part.astype(jnp.bfloat16)
        part_out[turn, away - 1, :, 1] = value_part.astype(jnp.bfloat16)
        pltpu.make_async_remote_copy(
            src_ref=part_out.at[turn, away - 1],
            dst_ref=part_in.at[turn, away - 1],
            send_sem=part_send.at[turn, away - 1],
            recv_sem=part_recv.at[turn, away - 1],
            device_id=partner(away),
            device_id_type=MESH,
        ).start()

    def pass_on(turn, key_part, value_part):
        for away in range(1, inner):
            arrived(part_in.at[turn, away - 1], part_recv.at[turn, away - 1])
            key_part = key_part + part_in[turn, away - 1, :, 0].astype(jnp.float32)
            value_part = value_part + part_in[turn, away - 1, :, 1].astype(jnp.float32)
        sum_out[turn, :, 0] = key_part.astype(jnp.bfloat16)
        sum_out[turn, :, 1] = value_part.astype(jnp.bfloat16)
        target = owner_side(turn)
        block = block_of(turn)

        for owner in range(shards):
            @pl.when(((owner != me) | (target != side)) & (owner < seen))
            def _():
                pltpu.make_async_remote_copy(
                    src_ref=sum_out.at[turn, owner],
                    dst_ref=sum_in.at[block, side * shards + me],
                    send_sem=sum_send.at[turn],
                    recv_sem=sum_recv.at[block],
                    device_id=(target * inner + core, owner),
                    device_id_type=MESH,
                ).start()

        @pl.when(target == side)
        def _():
            sum_in[block, side * shards + me] = sum_out[turn, me]

    order = order_of(inner, turns, per_section)
    take(*order[0])

    all_arrived(starts, start_recv, beside, range(1, 3))

    for away in range(1, outer):
        pl.semaphore_signal(side_ready, inc=1, device_id=across(away), device_id_type=MESH)
    loads[3].wait()
    query_pos = q_start[0] + lax.broadcasted_iota(jnp.int32, (slab, rows), 1)

    @pl.loop(0, shards)
    def _(slot):
        key_pos = starts[slot] + lax.broadcasted_iota(jnp.int32, (slab, rows), 0)
        bias[slot] = jnp.where(key_pos <= query_pos, 0.0, HIDDEN)

    for load in loads[:3]:
        load.wait()

    ready = outer == 1
    for index, (turn, away) in enumerate(order):
        if index:
            take(turn, away)
        parts = back(turn, away, front(turn, away))
        if away:
            hand_in(turn, away, *parts)
            continue
        if not ready:
            pl.semaphore_wait(side_ready, outer - 1)
            ready = True
        pass_on(turn, *parts)

    for head in range(KV_HEADS):
        keys = pairs[head, :, 0].reshape(total_keys, HEAD_DIM)
        for member in range(GROUP):
            query_head = head * GROUP + member
            columns = pl.ds(query_head * HEAD_DIM, HEAD_DIM)
            dq_all[:, columns] = contract(ds_all[query_head], keys, 0, 0) * SCALE

    all_arrived(starts, start_send, beside, range(1, 3))
    for turn in range(turns):
        if turn == turns - 1 or outer == 1:
            all_arrived(pairs.at[0], pair_send.at[turn], shards - reader - 1, range(1, shards))
        for away in range(1, inner):
            arrived(pairs.at[0], hop_send.at[turn, away])
            arrived(part_out.at[0, 0], part_send.at[turn, away - 1])
        sent = seen - (owner_side(turn) == side).astype(jnp.int32)
        all_arrived(sum_out.at[turn], sum_send.at[turn], sent, range(1, shards + 1))

    for block in range(per_section):
        counts = range(2 * outer - 1, outer * shards, outer)
        all_arrived(sum_in.at[block], sum_recv.at[block], outer * (shards - reader) - 1, counts)
        columns = pl.ds(block * HEAD_DIM, HEAD_DIM)
        arrivals = sum_in[block].astype(jnp.float32)
        dk_out[:, columns] = jnp.sum(arrivals[:, 0], axis=0) * SCALE
        dv_out[:, columns] = jnp.sum(arrivals[:, 1], axis=0)


def write_out(dq_all, dk_all, dv_all, dq_hbm, dk_hbm, dv_hbm, sems):
    rows = dq_all.shape[0] // WRITES
    copies = [
        pltpu.make_async_copy(dk_all, dk_hbm, sems.at[WRITES]),
        pltpu.make_async_copy(dv_all, dv_hbm, sems.at[WRITES + 1]),
    ]
    for part in range(WRITES):
        span = pl.ds(part * rows, rows)
        copies.append(pltpu.make_async_copy(dq_all.at[span], dq_hbm.at[0, span], sems.at[part]))
    for copy in copies:
        copy.start()
    for copy in copies:
        copy.wait()


def per_device(
    sections, shards, queries, out_grads, logsumexp, shared_keys, shared_values, query_starts, slab_starts
):
    rows, width = queries.shape[1], queries.shape[2]
    slab, kv_width = shared_keys.shape
    heads = logsumexp.shape[1]
    inner = inner_factor(sections)
    outer = sections // inner
    turns = KV_HEADS // inner
    per_section = KV_HEADS // sections
    half, full = jnp.bfloat16, jnp.float32
    stack = (shards, 2, slab, HEAD_DIM)
    dma = pltpu.SemaphoreType.DMA
    hbm = pl.BlockSpec(memory_space=pl.ANY)
    vmem = pl.BlockSpec(memory_space=pltpu.VMEM)
    share = (slab, kv_width // sections)
    results = (((rows, width), full), (share, full), (share, full))
    grads = pl.pallas_call(
        functools.partial(kernel, sections, shards),
        out_shape=tuple(pltpu.VMEM(*result) for result in results),
        in_specs=[hbm] * 7,
        out_specs=(vmem, vmem, vmem),
        scratch_shapes=[
            pltpu.VMEM((rows, width), half),
            pltpu.VMEM((rows, width), half),
            pltpu.VMEM((heads, rows), full),
            pltpu.VMEM((KV_HEADS,) + stack, half),
            pltpu.VMEM((shards, 1, rows), jnp.int32),
            pltpu.VMEM((shards, slab, rows), full),
            pltpu.VMEM((heads, shards * slab, rows), half),
            pltpu.VMEM((turns, max(inner - 1, 1)) + stack, half),
            pltpu.VMEM((turns, max(inner - 1, 1)) + stack, half),
            pltpu.VMEM((turns,) + stack, half),
            pltpu.VMEM((per_section, outer * shards) + stack[1:], half),
            pltpu.SMEM((1,), jnp.int32),
            pltpu.SMEM((1,), jnp.int32),
            dma((5,)),
            dma,
            dma,
            dma,
            dma((turns,)),
            dma((turns,)),
            dma((turns, inner)),
            dma((turns, inner)),
            dma((turns, max(inner - 1, 1))),
            dma((turns, max(inner - 1, 1))),
            dma((turns,)),
            dma((per_section,)),
            pltpu.SemaphoreType.REGULAR,
        ],
        compiler_params=pltpu.CompilerParams(
            collective_id=0, has_side_effects=True, vmem_limit_bytes=56 * 2**20
        ),
    )(queries, out_grads, logsumexp, shared_keys, shared_values, query_starts, slab_starts)
    return pl.pallas_call(
        write_out,
        out_shape=(
            jax.ShapeDtypeStruct((1, rows, width), full),
            jax.ShapeDtypeStruct(share, full),
            jax.ShapeDtypeStruct(share, full),
        ),
        in_specs=[vmem, vmem, vmem],
        out_specs=(hbm, hbm, hbm),
        scratch_shapes=[dma((WRITES + 2,))],
    )(*(pltpu.with_memory_space_constraint(grad, pltpu.VMEM) for grad in grads))


def solution(mesh):
    return jax.shard_map(
        functools.partial(per_device, mesh.shape["section"], mesh.shape["seq"]),
        mesh=mesh,
        in_specs=(
            P("section", "seq", None),
            P("section", "seq", None),
            P("section", None, "seq"),
            P("seq", None),
            P("seq", None),
            P("seq"),
            P("seq"),
        ),
        out_specs=(P("section", "seq", None), P("seq", "section"), P("seq", "section")),
        check_vma=False,
    )
```
